256 devices in a mesh: gy: 8 (over z), gz: 32 (over y, x, core).
Axes of the slice: x: 4, y: 4, z: 8, core: 2. Of those that a mesh axis runs over, the one named last changes fastest.
Arguments:
- scalar: float32 [1024, 512, 128], P('gz', 'gy'), may hold values from -6 to 6
- velocity: bfloat16 [3, 1024, 512, 128], P(None, 'gz', 'gy'), may hold values from -4 to 4
- row_shift: int32 [1024], P('gz'), may hold values from 0 to 32, as said below
- frac_index: int32 [1024], P('gz'), may hold values from 0 to 7
- brick_rank: int32 [32], replicated, may hold values from 0 to 31, each once
- color_coeffs: float32 [3, 4], replicated, may hold values from -1 to 1
- extinction: float32 [2], replicated, may hold values from 0.5 to 2
Outputs:
- field: float32 [1024, 512, 128], P('gz', 'gy')
- image: float32 [4, 512, 128], P(None, 'gy', 'gz')
The draws below stay inside these ranges and needn't reach their ends.
Inputs may be any that keep to these rules, and one draw needn't show every extreme that they name: `row_shift`: some slice is shifted by exactly 32 rows in every draw. `brick_rank`: a permutation of the brick indices.
All inputs are finite; a program needn't handle non-finite values.
Results may differ from the reference program's by a relative error of at most 0.0003.
Values may be sent and summed in bfloat16 or wider, within the bound.
No kernel may reach another device: no remote copies, remote signals or barrier semaphores. Data moves between devices by JAX's collectives and lax.ppermute only.
A program may use at most 64 MiB of HBM per device.

```python
import math
import jax
import jax.numpy as jnp
from jax import lax

CX = 128
CZ = 32
NFRAC = 8
SHIFT_MAX = 32
NY = 512
NZ = 1024
NBRICK = 32


def draw_row_shift(key, part):
    values = jax.random.randint(key, (NZ,), 0, SHIFT_MAX + 1)
    target = jax.random.randint(jax.random.fold_in(key, 7), (), 0, NZ)
    return values.at[target].set(SHIFT_MAX).astype(jnp.int32)


def touch_ends(drawn, own_key, smallest, high):
    longest = drawn.shape.index(max(drawn.shape))
    spots = []
    for shift in (0, 1):
        where = [jax.random.randint(jax.random.fold_in(own_key, axis), (), 0, length) for axis, length in enumerate(drawn.shape)]
        where[longest] = (where[longest] + shift) % drawn.shape[longest]
        spots.append(tuple(where))
    return drawn.at[spots[0]].set(smallest).at[spots[1]].set(high)


def steps_of(key, extent, cuts, low, largest):
    factor_of, own = 1.0, jax.random.fold_in(key, 6)
    for dim, shards_of in cuts:
        heights = jnp.exp(jax.random.uniform(jax.random.fold_in(own, dim), (shards_of,), jnp.float32, low / len(cuts), largest / len(cuts)))
        factor_of = factor_of * jnp.repeat(heights, extent[dim] // shards_of).reshape([-1 if axis == dim else 1 for axis in range(len(extent))])
    return factor_of


def scatter_about(key, extent, spread, bound, split=(), dtype=jnp.bfloat16):
    entries = spread * jax.random.normal(key, extent, jnp.float32)
    if split:
        entries = entries * steps_of(key, extent, split, -0.22, 0.18)
    return jnp.clip(entries, -bound, bound).astype(dtype)


def setup_inputs(seed: int = 0) -> dict:
    seeds = jax.random.split(jax.random.key(seed), 8)
    scalar = scatter_about(seeds[0], (NZ, NY, CX), 1.0, 6.0, ((0, 32), (1, 8)), jnp.float32)
    velocity = scatter_about(seeds[1], (3, NZ, NY, CX), 1.0, 4.0, ((1, 32), (2, 8)))
    row_shift = draw_row_shift(jax.random.fold_in(seeds[7], 71), 0)
    frac_index = touch_ends(jax.random.randint(seeds[3], (NZ,), 0, NFRAC), jax.random.fold_in(seeds[3], 1), 0, NFRAC - 1).astype(jnp.int32)
    brick_rank = jax.random.permutation(seeds[4], NBRICK).astype(jnp.int32)
    color_coeffs = jnp.clip(jax.random.uniform(seeds[5], (3, 4), jnp.float32, -1.0, 1.0), -1.0, 1.0)
    extinction = jnp.clip(jnp.exp(jax.random.uniform(seeds[6], (2,), jnp.float32, math.log(0.5), math.log(2.0))), 0.5, 2.0)
    return {"scalar": scalar, "velocity": velocity, "row_shift": row_shift, "frac_index": frac_index, "brick_rank": brick_rank, "color_coeffs": color_coeffs, "extinction": extinction}


diffusivity = 0.05
time_step = 0.2


def tendency(padded, velocity):
    wide = jnp.pad(padded, ((0, 0), (0, 0), (1, 1)))
    centre = wide[1:-1, 1:-1, 1:-1]
    z_next = wide[2:, 1:-1, 1:-1]
    z_prev = wide[:-2, 1:-1, 1:-1]
    y_next = wide[1:-1, 2:, 1:-1]
    y_prev = wide[1:-1, :-2, 1:-1]
    x_next = wide[1:-1, 1:-1, 2:]
    x_prev = wide[1:-1, 1:-1, :-2]
    flow = velocity.astype(jnp.float32)
    advection = 0.5 * (flow[0] * (z_next - z_prev) + flow[1] * (y_next - y_prev) + flow[2] * (x_next - x_prev))
    laplacian = z_next + z_prev + y_next + y_prev + x_next + x_prev - 6.0 * centre
    return diffusivity * laplacian - advection


def pad_faces(values):
    return jnp.pad(values, ((1, 1), (1, 1), (0, 0)))


def shear_slices(joined, row_shift, frac_index, margin, height):
    fraction = frac_index.astype(jnp.float32) / NFRAC

    def one_slice(slab, offset, weight):
        start = (margin + 1 - offset).astype(jnp.int32)
        nearer = lax.dynamic_slice_in_dim(slab, start, height, 0)
        farther = lax.dynamic_slice_in_dim(slab, start - 1, height, 0)
        return (1.0 - weight) * nearer + weight * farther

    return jax.vmap(one_slice)(joined, row_shift, fraction)


def brick_light(values, color_coeffs, extinction, slice_depth):
    channels = []
    for colour_index in range(3):
        coeffs = color_coeffs[colour_index]
        channels.append(coeffs[0] + values * (coeffs[1] + values * (coeffs[2] + values * coeffs[3])))
    emission = jnp.stack(channels, 0)
    optical = (extinction[0] * values * values + extinction[1]) * slice_depth
    before = jnp.cumsum(optical, axis=0) - optical
    weights = jnp.exp(-before) * (1.0 - jnp.exp(-optical))
    colour = jnp.sum(weights[None] * emission, axis=1)
    depth = jnp.sum(optical, axis=0)
    return colour, depth


def composite(colour, depth, brick_rank):
    precede = (brick_rank[:, None] < brick_rank[None, :]).astype(jnp.float32)
    earlier = jnp.einsum("jk,jyx->kyx", precede, depth, precision=lax.Precision.HIGHEST)
    shaded = jnp.sum(jnp.exp(-earlier)[:, None] * colour, axis=0)
    opacity = 1.0 - jnp.exp(-jnp.sum(depth, axis=0))
    return jnp.concatenate([shaded, opacity[None]], 0)


def reference(scalar, velocity, row_shift, frac_index, brick_rank, color_coeffs, extinction):
    first = scalar + time_step * tendency(pad_faces(scalar), velocity)
    second = 0.75 * scalar + 0.25 * (first + time_step * tendency(pad_faces(first), velocity))
    field = (1.0 / 3.0) * scalar + (2.0 / 3.0) * (second + time_step * tendency(pad_faces(second), velocity))
    joined = jnp.pad(field, ((0, 0), (SHIFT_MAX + 1, 0), (0, 0)))
    sheared = shear_slices(joined, row_shift, frac_index, SHIFT_MAX, NY)
    bricks = sheared.reshape(NBRICK, CZ, NY, CX)
    slice_depth = 1.0 / NZ
    colour, depth = lax.map(lambda brick: brick_light(brick, color_coeffs, extinction, slice_depth), bricks)
    image = composite(colour, depth, brick_rank)
    return field, image
```

```python
import jax
import jax.numpy as jnp
import numpy as np
from jax import lax
from jax.experimental import pallas as pl
from jax.experimental.pallas import tpu as pltpu
from jax.sharding import PartitionSpec as P

NFRAC = 8
SHIFT_MAX = 32
CZ, CY, CX = 32, 64, 128
PZ = 40
PLANE = CY
SS_ROWS = PZ * PLANE + 16
UU_PLANE = PZ * PLANE
TOP = SHIFT_MAX + 1
SH_ROWS = CZ * TOP
F32, BF16, I16 = jnp.float32, jnp.bfloat16, jnp.int16
VM = pl.BlockSpec(memory_space=pltpu.VMEM)
SM = pl.BlockSpec(memory_space=pltpu.SMEM)


def params():
    return pltpu.CompilerParams(vmem_limit_bytes=24 * 1024 * 1024)


def call(kernel, outs, n_smem, n_vmem, scratch=(), aliases=None, cost=(1000000, 1000000)):
    return pl.pallas_call(
        kernel,
        out_shape=outs,
        in_specs=[SM] * n_smem + [VM] * n_vmem,
        out_specs=jax.tree.map(lambda _: VM, outs),
        scratch_shapes=list(scratch),
        input_output_aliases=aliases or {},
        compiler_params=params(),
        cost_estimate=pl.CostEstimate(flops=cost[0], bytes_accessed=cost[1], transcendentals=0),
    )


def shaped(shape, dtype):
    return jax.ShapeDtypeStruct(shape, dtype)


def shifted(value, axis, by):
    count = lax.axis_size(axis)
    pairs = [(i, i + by) for i in range(count) if 0 <= i + by < count]
    return lax.ppermute(value, axis, pairs)


def split(value):
    high = value.astype(BF16)
    return high, (value - high.astype(F32)).astype(BF16)


def pack_z(s_ref, u_ref, up_ref, down_ref):
    for out, s_lo, u_lo in ((up_ref, CZ - 3, CZ - 2), (down_ref, 0, 0)):
        high, low = split(s_ref[s_lo : s_lo + 3].reshape(3 * CY, CX))
        out[0 : 3 * CY] = high
        out[3 * CY : 6 * CY] = low
        for comp in range(3):
            out[(6 + 2 * comp) * CY : (8 + 2 * comp) * CY] = u_ref[comp, u_lo : u_lo + 2].reshape(2 * CY, CX)


def flat(z):
    return 8 + PLANE * (z + 4)


def assemble(s_ref, u_ref, below_ref, above_ref, ss_ref, uu_ref, up_ref, down_ref, face):
    ss_ref[0:8] = jnp.zeros((8, CX), F32)
    ss_ref[SS_ROWS - 8 : SS_ROWS] = jnp.zeros((8, CX), F32)
    for z in (-4, CZ + 3):
        ss_ref[flat(z) : flat(z) + CY] = jnp.zeros((CY, CX), F32)
    for halo, z in ((below_ref, -3), (above_ref, CZ)):
        ss_ref[flat(z) : flat(z) + 3 * CY] = halo[0 : 3 * CY].astype(F32) + halo[3 * CY : 6 * CY].astype(F32)

    def copy_plane(z, _):
        base = pl.multiple_of(flat(z), 8)
        ss_ref[pl.ds(base, CY)] = s_ref[z]
        for comp in range(3):
            base = pl.multiple_of(comp * UU_PLANE + PLANE * (z + 4), 8)
            uu_ref[pl.ds(base, CY)] = u_ref[comp, z].astype(F32)
        return 0

    lax.fori_loop(0, CZ, copy_plane, 0, unroll=2)
    for comp in range(3):
        for halo, z in ((below_ref, -2), (above_ref, CZ)):
            base = comp * UU_PLANE + PLANE * (z + 4)
            uu_ref[base : base + 2 * CY] = halo[(6 + 2 * comp) * CY : (8 + 2 * comp) * CY].astype(F32)
        for z in (-4, -3, CZ + 2, CZ + 3):
            base = comp * UU_PLANE + PLANE * (z + 4)
            uu_ref[base : base + CY] = jnp.zeros((CY, CX), F32)
    for out, s_lo, u_lo in ((up_ref, CY - 3, CY - 2), (down_ref, 0, 0)):
        for row in range(3):
            value = ss_ref[pl.ds(8 + s_lo + row, PZ, stride=PLANE)]
            high = value.astype(BF16).astype(F32)
            face[row * PZ : (row + 1) * PZ] = high
            face[(3 + row) * PZ : (4 + row) * PZ] = value - high
        for comp in range(3):
            for row in range(2):
                at = 6 + 2 * comp + row
                face[at * PZ : (at + 1) * PZ] = uu_ref[pl.ds(comp * UU_PLANE + u_lo + row, PZ, stride=PLANE)]
        out[...] = face[...].astype(BF16)


def advance(c, zn, zp, yn, yp, uz, uy, ux, lane):
    rows = c.shape[0]
    xn = jnp.where(lane == CX - 1, 0.0, pltpu.roll(c, CX - 1, 1))
    xp = jnp.where(lane == 0, 0.0, pltpu.roll(c, 1, 1))
    total = (zn + zp) + (yn + yp) + (xn + xp)
    flow = uz * (zn - zp) + uy * (yn - yp) + ux * (xn - xp)
    return 0.94 * c + (0.01 * total - 0.1 * flow)


CHUNK = 16


def stencil(edge_ref, ss_ref, uu_ref, field_ref, f1, f2):
    lane = lax.broadcasted_iota(jnp.int32, (CHUNK, CX), 1)

    def sweep(src, z_lo, z_hi, put):
        def plane(z, _):
            base = pl.multiple_of(flat(z), 8)
            near = src.at[pl.ds(pl.multiple_of(base - 8, 8), CY + 16)]
            after = src.at[pl.ds(pl.multiple_of(base + PLANE, 8), CY)]
            before = src.at[pl.ds(pl.multiple_of(base - PLANE, 8), CY)]
            vel = [uu_ref.at[pl.ds(pl.multiple_of(comp * UU_PLANE + base - 8, 8), CY)] for comp in range(3)]
            for k in range(0, CY, CHUNK):
                here = slice(k, k + CHUNK)
                value = advance(
                    near[8 + k : 8 + k + CHUNK],
                    after[here],
                    before[here],
                    near[9 + k : 9 + k + CHUNK],
                    near[7 + k : 7 + k + CHUNK],
                    *[v[here] for v in vel],
                    lane,
                )
                put(z, base, k, value)
            return 0

        lax.fori_loop(z_lo, z_hi, plane, 0, unroll=2)

    def put_first(z, base, k, value):
        f1[pl.ds(pl.multiple_of(base + k, 8), CHUNK)] = value

    def put_second(z, base, k, value):
        at = pl.multiple_of(base + k, 8)
        f2[pl.ds(at, CHUNK)] = 0.75 * ss_ref[pl.ds(at, CHUNK)] + 0.25 * value

    def put_field(z, base, k, value):
        at = pl.multiple_of(base + k, 8)
        field_ref[z, pl.ds(k, CHUNK), :] = (1.0 / 3.0) * ss_ref[pl.ds(at, CHUNK)] + (2.0 / 3.0) * value

    def mask(dst, width):
        for z, side in ((-width, 0), (CZ, 1)):
            rows = slice(flat(z), flat(z) + width * CY)
            dst[rows] = dst[rows] * edge_ref[side]

    sweep(ss_ref, -2, CZ + 2, put_first)
    mask(f1, 2)
    sweep(f1, -1, CZ + 1, put_second)
    mask(f2, 1)
    sweep(f2, 0, CZ, put_field)


def powers_of_two():
    return jnp.asarray((2.0 ** (np.arange(128) - 110.0)).astype(np.float32).reshape(1, 128))


def edges(edge_ref, pow_ref, ss_ref, uu_ref, below_ref, above_ref, old_ref, field_ref, shear_ref, face, se, ue, fe, ge, top):
    lane = lax.broadcasted_iota(jnp.int32, (PZ, CX), 1)
    spot = lax.broadcasted_iota(jnp.int32, (PZ, CX), 0)
    z_mask = jnp.where(spot < 4, edge_ref[0], jnp.where(spot >= 4 + CZ, edge_ref[1], 1.0))
    field_ref[...] = old_ref[...]

    def at(row):
        return 8 + row * PZ

    for side in (0, 1):
        halo = (below_ref, above_ref)[side]
        face[...] = halo[...].astype(F32)
        own = range(0, 6) if side == 0 else range(CY - 6, CY)
        first_own = 3 if side == 0 else 0
        first_halo = 0 if side == 0 else 6
        for n, y in enumerate(own):
            r = at(first_own + n)
            se[r : r + PZ] = ss_ref[pl.ds(8 + y, PZ, stride=PLANE)]
        for n in range(3):
            r = at(first_halo + n)
            se[r : r + PZ] = face[n * PZ : (n + 1) * PZ] + face[(3 + n) * PZ : (4 + n) * PZ]
        for comp in range(3):
            for n in range(7):
                r = (comp * 7 + n) * PZ
                face_row = n + 1
                if first_own <= face_row < first_own + 6:
                    y = own[face_row - first_own]
                    ue[r : r + PZ] = uu_ref[pl.ds(comp * UU_PLANE + y, PZ, stride=PLANE)]
                else:
                    m = (face_row - 1) if side == 0 else (face_row - 6)
                    q = (6 + 2 * comp + m) * PZ
                    ue[r : r + PZ] = face[q : q + PZ]

        def value_at(src, row):
            r = at(row)
            return advance(
                src[r : r + PZ],
                src[r + 1 : r + 1 + PZ],
                src[r - 1 : r - 1 + PZ],
                src[r + PZ : r + 2 * PZ],
                src[r - PZ : r],
                *[ue[(comp * 7 + row - 1) * PZ : (comp * 7 + row) * PZ] for comp in range(3)],
                lane,
            )

        def outside(row):
            return row < 3 if side == 0 else row >= 6

        for row in range(1, 8):
            value = value_at(se, row) * z_mask
            if outside(row):
                value = value * edge_ref[2 + side]
            fe[at(row) : at(row) + PZ] = value
        for row in range(2, 7):
            value = 0.75 * se[at(row) : at(row) + PZ] + 0.25 * value_at(fe, row)
            value = value * z_mask
            if outside(row):
                value = value * edge_ref[2 + side]
            ge[at(row) : at(row) + PZ] = value
        for row in range(3, 6):
            value = (1.0 / 3.0) * se[at(row) : at(row) + PZ] + (2.0 / 3.0) * value_at(ge, row)
            y = row - 3 if side == 0 else CY - 6 + row
            fe[at(row) : at(row) + PZ] = value
            for z in range(CZ):
                field_ref[z, y : y + 1, :] = fe[at(row) + 4 + z : at(row) + 5 + z]

    peak = jnp.zeros((8, CX), F32)
    for z in range(CZ):
        rows = field_ref[z, CY - TOP : CY, :]
        top[z * TOP : (z + 1) * TOP] = rows
        part = jnp.abs(field_ref[z, CY - TOP + 1 : CY, :])
        for k in range(0, TOP - 1, 8):
            peak = jnp.maximum(peak, part[k : k + 8])
        peak = jnp.maximum(peak, jnp.abs(rows[0:1]))
    most = jnp.max(peak)
    scales = pow_ref[...]
    step = jnp.sum((most > scales).astype(F32))
    index = lax.broadcasted_iota(jnp.int32, (1, CX), 1).astype(F32)
    scale = jnp.sum(jnp.where(index == step, scales, 0.0))
    shear_ref[0:SH_ROWS] = jnp.round(top[...] * (32000.0 / scale)).astype(I16)
    shear_ref[SH_ROWS : SH_ROWS + 16] = (jnp.zeros((16, CX), F32) + step).astype(I16)


def lights(shift_ref, frac_ref, color_ref, ext_ref, pow_ref, field_ref, shear_ref, out_ref, above, joined, turned):
    steps = shear_ref[SH_ROWS : SH_ROWS + 16].astype(F32)
    index = lax.broadcasted_iota(jnp.int32, (16, CX), 1).astype(F32)
    scale = jnp.max(jnp.where(index == steps, pow_ref[...], 0.0))
    above[0:SH_ROWS] = shear_ref[0:SH_ROWS].astype(F32) * (scale / 32000.0)
    for z in range(CZ):
        joined[z, 7:40, :] = above[z * TOP : (z + 1) * TOP]
        joined[z, 40:104, :] = field_ref[z]
    coeffs = [[color_ref[c, n] for n in range(4)] for c in range(3)]
    quad, const = ext_ref[0], ext_ref[1]
    HALF = 32
    for lo in range(0, CY, HALF):

        def one(z, state):
            trans, depth, red, green, blue = state
            start = 40 + lo - shift_ref[z]
            weight = frac_ref[z].astype(F32) * (1.0 / NFRAC)
            near = joined[z, pl.ds(start, HALF), :]
            far = joined[z, pl.ds(start - 1, HALF), :]
            g = (1.0 - weight) * near + weight * far
            optical = (quad * g * g + const) * (1.0 / 1024.0)
            fade = jnp.exp(-optical)
            share = trans * (1.0 - fade)
            sums = []
            for (a0, a1, a2, a3), total in zip(coeffs, (red, green, blue)):
                sums.append(total + share * (a0 + g * (a1 + g * (a2 + g * a3))))
            return (trans * fade, depth + optical, *sums)

        zero = jnp.zeros((HALF, CX), F32)
        _, depth, red, green, blue = lax.fori_loop(0, CZ, one, (zero + 1.0, zero, zero, zero, zero), unroll=2)
        for n, value in enumerate((red, green, blue, depth)):
            turned[n * CY + lo : n * CY + lo + HALF] = value
    for h in range(2):
        block = turned[h * 128 : (h + 1) * 128].T
        turned[h * 128 : (h + 1) * 128] = block
    for d in range(32):
        for h in range(2):
            out_ref[8 * d + 4 * h : 8 * d + 4 * h + 4] = turned[h * 128 + 4 * d : h * 128 + 4 * d + 4]


def finish(rank_ref, got_ref, image_ref, dep, order):
    for k in range(32):
        order[rank_ref[k]] = k
    got = got_ref[...].reshape(32, 8, 128)
    lane = lax.broadcasted_iota(jnp.int32, (32, 8, 128), 2)
    row = lax.broadcasted_iota(jnp.int32, (32, 8, 128), 1)
    depth = jnp.where(lane >= 64, got, pltpu.roll(got, 64, 2))
    depth = jnp.where(row >= 4, depth, pltpu.roll(depth, 4, 1))
    dep[...] = depth.reshape(256, 128)
    run = jnp.zeros((8, 128), F32)
    total = jnp.zeros((8, 128), F32)
    for r in range(32):
        base = pl.multiple_of(order[r] * 8, 8)
        total = total + jnp.exp(-run) * got_ref[pl.ds(base, 8)]
        run = run + dep[pl.ds(base, 8)]
    total = jnp.where((row[0] >= 4) & (lane[0] >= 64), 1.0 - jnp.exp(-run), total)
    for c in range(4):
        h, half = divmod(c, 2)
        image_ref[c] = total[4 * h : 4 * h + 4, 64 * half : 64 * half + 64]


def on_device(scalar, velocity, row_shift, frac_index, brick_rank, color_coeffs, extinction):
    gz, gy = lax.axis_index("gz"), lax.axis_index("gy")
    inside = jnp.stack([gz > 0, gz < lax.axis_size("gz") - 1, gy > 0, gy < lax.axis_size("gy") - 1]).astype(F32)
    pows = powers_of_two()

    z_face = shaped((12 * CY, CX), BF16)
    z_up, z_down = call(pack_z, (z_face, z_face), 0, 2)(scalar, velocity)
    z_below, z_above = shifted(z_up, "gz", 1), shifted(z_down, "gz", -1)

    y_face = shaped((12 * PZ, CX), BF16)
    ss, uu, y_up, y_down = call(
        assemble,
        (shaped((SS_ROWS, CX), F32), shaped((3 * UU_PLANE, CX), F32), y_face, y_face),
        0,
        4,
        [pltpu.VMEM((12 * PZ, CX), F32)],
    )(scalar, velocity, z_below, z_above)
    y_below, y_above = shifted(y_up, "gy", 1), shifted(y_down, "gy", -1)

    inner = call(
        stencil,
        shaped((CZ, CY, CX), F32),
        1,
        2,
        [pltpu.VMEM((SS_ROWS, CX), F32), pltpu.VMEM((SS_ROWS, CX), F32)],
        cost=(30000000, 6000000),
    )(inside, ss, uu)
    edge_rows = 9 * PZ + 16
    field, top = call(
        edges,
        (shaped((CZ, CY, CX), F32), shaped((SH_ROWS + 16, CX), I16)),
        1,
        6,
        [
            pltpu.VMEM((12 * PZ, CX), F32),
            pltpu.VMEM((edge_rows, CX), F32),
            pltpu.VMEM((21 * PZ, CX), F32),
            pltpu.VMEM((edge_rows, CX), F32),
            pltpu.VMEM((edge_rows, CX), F32),
            pltpu.VMEM((SH_ROWS, CX), F32),
        ],
    )(inside, pows, ss, uu, y_below, y_above, inner)
    above = shifted(top, "gy", 1)

    sent = call(
        lights,
        shaped((256, CX), F32),
        4,
        3,
        [
            pltpu.VMEM((SH_ROWS, CX), F32),
            pltpu.VMEM((CZ, 104, CX), F32),
            pltpu.VMEM((256, CX), F32),
        ],
    )(row_shift, frac_index, color_coeffs, extinction, pows, field, above)
    got = lax.all_to_all(sent.reshape(32, 8, CX), "gz", split_axis=0, concat_axis=0, tiled=True)

    image = call(
        finish,
        shaped((4, 4, CY), F32),
        1,
        1,
        [pltpu.VMEM((256, CX), F32), pltpu.SMEM((32,), jnp.int32)],
    )(brick_rank, got.reshape(256, CX))
    return field, jnp.transpose(image, (0, 2, 1))


def solution(mesh):
    placed = (P("gz", "gy", None), P(None, "gz", "gy", None), P("gz"), P("gz"), P(), P(), P())
    return jax.shard_map(
        on_device,
        mesh=mesh,
        in_specs=placed,
        out_specs=(P("gz", "gy", None), P(None, "gy", "gz")),
        check_vma=False,
    )
```

```python
import jax
import jax.numpy as jnp
import numpy as np
from jax import lax
from jax.experimental import pallas as pl
from jax.experimental.pallas import tpu as pltpu
from jax.sharding import PartitionSpec as P


NFRAC = 8
SHIFT_MAX = 32
CZ, CY, CX = 32, 64, 128
PZ = 40
PLANE = CY
SS_ROWS = PZ * PLANE + 16
CELLS = CZ * CY
UE_ROWS = 6 * PZ * 8
J_ROWS = 80
UP, DOWN = 6, 3
UP_ROWS, DOWN_ROWS = 1088, 480
TOP = SHIFT_MAX + 1 - 3
SH_ROWS = CZ * TOP
F32, BF16, I16 = jnp.float32, jnp.bfloat16, jnp.int16
VM = pl.BlockSpec(memory_space=pltpu.VMEM)
SM = pl.BlockSpec(memory_space=pltpu.SMEM)
HB = pl.BlockSpec(memory_space=pltpu.HBM)


def call(kernel, outs, ins, scratch=(), aliases=None, out_specs=None, cycles=1000, vmem=16777216):
    return pl.pallas_call(
        kernel,
        out_shape=outs,
        in_specs=list(ins),
        out_specs=out_specs or jax.tree.map(lambda _: VM, outs),
        scratch_shapes=list(scratch),
        input_output_aliases=aliases or {},
        compiler_params=pltpu.CompilerParams(vmem_limit_bytes=vmem),
        cost_estimate=pl.CostEstimate(flops=4096 * cycles, bytes_accessed=1024 * cycles, transcendentals=0),
    )


def shaped(shape, dtype):
    return jax.ShapeDtypeStruct(shape, dtype)


def shifted(value, axis, by):
    count = lax.axis_size(axis)
    pairs = [(i, i + by) for i in range(count) if 0 <= i + by < count]
    return lax.ppermute(value, axis, pairs)


def split(value):
    high = value.astype(BF16)
    return high, (value - high.astype(F32)).astype(BF16)


def powers_of_two():
    return jnp.asarray(np.repeat((2.0 ** (np.arange(128) - 110.0)).astype(np.float32)[:, None], CX, 1))


def pack_z(s_ref, u_ref, up_ref, down_ref, s_buf, u_buf, sem):
    copies = []
    for side, (s_lo, u_lo) in enumerate(((CZ - 3, CZ - 2), (0, 0))):
        copies.append(pltpu.make_async_copy(s_ref.at[pl.ds(s_lo * CY, 3 * CY)], s_buf.at[side], sem.at[2 * side]))
        copies.append(pltpu.make_async_copy(u_ref.at[:, pl.ds(u_lo, 2)], u_buf.at[side], sem.at[2 * side + 1]))
    for copy in copies:
        copy.start()
    for side, out in enumerate((up_ref, down_ref)):
        copies[2 * side].wait()
        high, low = split(s_buf[side])
        out[0 : 3 * CY] = high
        out[3 * CY : 6 * CY] = low
        copies[2 * side + 1].wait()
        for comp in range(3):
            out[(6 + 2 * comp) * CY : (8 + 2 * comp) * CY] = u_buf[side, comp].reshape(2 * CY, CX)


def flat(z):
    return 8 + PLANE * (z + 4)


def aligned(x):
    return x if isinstance(x, int) else pl.multiple_of(x, 8)


def advance(c, zn, zp, yn, yp, uz, uy, ux, lane):
    xn = jnp.where(lane == CX - 1, 0.0, pltpu.roll(c, CX - 1, 1))
    xp = jnp.where(lane == 0, 0.0, pltpu.roll(c, 1, 1))
    total = (zn + zp) + (yn + yp) + (xn + xp)
    flow = uz * (zn - zp) + uy * (yn - yp) + ux * (xn - xp)
    return 0.94 * c + (0.01 * total - 0.1 * flow)


FULL = ((0, 16), (16, 16), (32, 16), (48, 16))
UPPER = ((24, 8), (32, 16), (48, 16))
UPPER_2, LOWER_2 = ((16, 16), (32, 16), (48, 16)), ((0, 16),)
EARLY = 14
LOWER = ((0, 16), (16, 8))


def one_plane(src, z, u_of, put, chunks=FULL):
    base = aligned(flat(z))
    near = src.at[pl.ds(aligned(base - 8), CY + 16)]
    after = src.at[pl.ds(aligned(base + PLANE), CY)]
    before = src.at[pl.ds(aligned(base - PLANE), CY)]
    for k, n in chunks:
        lane = lax.broadcasted_iota(jnp.int32, (n, CX), 1)
        value = advance(
            near[8 + k : 8 + k + n],
            after[k : k + n],
            before[k : k + n],
            near[9 + k : 9 + k + n],
            near[7 + k : 7 + k + n],
            *[u_of(comp, k, n).astype(F32) for comp in range(3)],
            lane,
        )
        put(aligned(base + k), k, n, value)


def run_planes(lo, hi, step, body):
    trips = (hi - lo) // step

    def group(i, _):
        for n in range(step):
            body(lo + i * step + n)
        return 0

    lax.fori_loop(0, trips, group, 0)
    for z in range(lo + trips * step, hi):
        body(z)


def own_velocity(u_ref, z):
    return lambda comp, k, n: u_ref[comp, z, k : k + n, :]


def any_velocity(u_ref, below_ref, above_ref, z):
    if 0 <= z < CZ:
        return own_velocity(u_ref, z)
    ref, plane = (below_ref, z + 2) if z < 0 else (above_ref, z - CZ)

    def of(comp, k, n):
        base = (6 + 2 * comp + plane) * CY + k
        return ref[base : base + n]

    return of


def put_first(f1):
    def put(at, k, n, value):
        f1[pl.ds(at, n)] = value

    return put


def put_second(f2, ss_ref):
    def put(at, k, n, value):
        f2[pl.ds(at, n)] = 0.75 * ss_ref[pl.ds(at, n)] + 0.25 * value

    return put


def put_field(field_ref, ss_ref):
    def put(at, k, n, value):
        to = aligned(at - flat(0))
        field_ref[pl.ds(to, n)] = (1.0 / 3.0) * ss_ref[pl.ds(at, n)] + (2.0 / 3.0) * value

    return put


GROUP = 8


def inner(s_ref, u_ref, ss_ref, uv_ref, ue_ref, f1, f2, sem):
    copies = []
    for c in range(CZ // GROUP):
        rows = GROUP * CY
        copies.append(
            (
                pltpu.make_async_copy(s_ref.at[pl.ds(c * rows, rows)], ss_ref.at[pl.ds(flat(0) + c * rows, rows)], sem.at[2 * c]),
                pltpu.make_async_copy(u_ref.at[:, pl.ds(c * GROUP, GROUP)], uv_ref.at[:, pl.ds(c * GROUP, GROUP)], sem.at[2 * c + 1]),
            )
        )
    for pair in copies:
        for copy in pair:
            copy.start()

    def take(z):
        for comp in range(3):
            for side, k in ((0, 0), (1, CY - 16)):
                rows = uv_ref[comp, z, k : k + 16, :].astype(F32)
                to = ((2 * comp + side) * PZ + 4 + z) * 8
                ue_ref[pl.ds(aligned(to), 8)] = rows[8 * side : 8 * side + 8]

    for c, pair in enumerate(copies):
        for copy in pair:
            copy.wait()
        lo, hi = max(1, GROUP * c - 1), GROUP * (c + 1) - 1
        run_planes(lo, hi, 4, lambda z: one_plane(ss_ref, z, own_velocity(uv_ref, z), put_first(f1)))
        run_planes(GROUP * c, GROUP * (c + 1), 4, take)
    run_planes(2, EARLY, 4, lambda z: one_plane(f1, z, own_velocity(uv_ref, z), put_second(f2, ss_ref), UPPER_2))


def assemble(below_ref, above_ref, ss_in, ue_in, ss_ref, ue_ref, up_ref, down_ref, face):
    for halo, z in ((below_ref, -3), (above_ref, CZ)):
        ss_ref[flat(z) : flat(z) + 3 * CY] = halo[0 : 3 * CY].astype(F32) + halo[3 * CY : 6 * CY].astype(F32)
    for comp in range(3):
        for halo, z in ((below_ref, -2), (above_ref, CZ)):
            for n in range(2):
                base = (6 + 2 * comp + n) * CY
                for side, k in ((0, 0), (1, CY - 16)):
                    rows = halo[base + k : base + k + 16].astype(F32)
                    to = ((2 * comp + side) * PZ + 4 + z + n) * 8
                    ue_ref[to : to + 8] = rows[8 * side : 8 * side + 8]
    for side, out, count, s_lo in ((1, up_ref, UP, CY - UP), (0, down_ref, DOWN, 0)):
        for row in range(count):
            value = ss_ref[pl.ds(8 + s_lo + row, PZ, stride=PLANE)]
            high = value.astype(BF16).astype(F32)
            face[row * PZ : (row + 1) * PZ] = high
            face[(count + row) * PZ : (count + row + 1) * PZ] = value - high
        for comp in range(3):
            for row in range(count - 1):
                at = 2 * count + (count - 1) * comp + row
                start = (2 * comp + side) * PZ * 8 + (8 - (count - 1) if side else 0) + row
                face[at * PZ : (at + 1) * PZ] = ue_ref[pl.ds(start, PZ, stride=8)]
        out[...] = face[0 : out.shape[0]].astype(BF16)


def inside(axis, side):
    place = lax.axis_index(axis)
    return jnp.where(place == (lax.axis_size(axis) - 1) * side, 0.0, 1.0)


def middle(pow_ref, u_ref, below_ref, above_ref, ss_ref, f1_in, f2_in, f1, f2, field_ref, shear_ref, top):
    def velocity(z):
        return any_velocity(u_ref, below_ref, above_ref, z)

    def mask(dst, width):
        for z, side in ((-width, 0), (CZ, 1)):
            rows = slice(flat(z), flat(z) + width * CY)
            dst[rows] = dst[rows] * inside("gz", side)

    for z in (-2, -1, 0, CZ - 1, CZ, CZ + 1):
        one_plane(ss_ref, z, velocity(z), put_first(f1))
    mask(f1, 2)
    for z in (-1, 0, 1, CZ):
        one_plane(f1, z, velocity(z), put_second(f2, ss_ref), UPPER_2)
    run_planes(EARLY, CZ, 3, lambda z: one_plane(f1, z, own_velocity(u_ref, z), put_second(f2, ss_ref), UPPER_2))
    mask(f2, 1)
    run_planes(0, CZ, 4, lambda z: one_plane(f2, z, own_velocity(u_ref, z), put_field(field_ref, ss_ref), UPPER))
    for z in range(CZ):
        top[z * TOP : (z + 1) * TOP] = field_ref[z * CY + CY - TOP - 3 : (z + 1) * CY - 3]
    peak = jnp.max(jnp.abs(top[...]), axis=0, keepdims=True)
    enough = pow_ref[...] >= peak
    scale = jnp.min(jnp.where(enough, pow_ref[...], 2.0**17), axis=0, keepdims=True)
    step = jnp.sum(jnp.where(enough, 0.0, 1.0), axis=0, keepdims=True)
    shear_ref[0:SH_ROWS] = jnp.round(top[...] * (32000.0 / scale)).astype(I16)
    shear_ref[SH_ROWS : SH_ROWS + 16] = jnp.broadcast_to(step, (16, CX)).astype(I16)


def fix_rows(side, ss_ref, ue_ref, halo, field_ref, joined, face, se, fe, ge):
    count = (UP, DOWN)[side]
    first_own, first_halo, y_own, total = ((UP, 0, 0, UP + 6), (0, 6, CY - 6, 6 + DOWN))[side]
    lane = lax.broadcasted_iota(jnp.int32, (PZ, CX), 1)
    spot = lax.broadcasted_iota(jnp.int32, (PZ, CX), 0)
    z_mask = jnp.where(spot < 4, inside("gz", 0), jnp.where(spot >= 4 + CZ, inside("gz", 1), 1.0))
    y_mask = z_mask * inside("gy", side)
    face[0 : halo.shape[0]] = halo[...].astype(F32)

    def at(row):
        return 8 + row * PZ

    def beyond(row):
        return not first_own <= row < first_own + 6

    for n in range(6):
        r = at(first_own + n)
        se[r : r + PZ] = ss_ref[pl.ds(8 + y_own + n, PZ, stride=PLANE)]
    for n in range(count):
        r = at(first_halo + n)
        se[r : r + PZ] = face[n * PZ : (n + 1) * PZ] + face[(count + n) * PZ : (count + n + 1) * PZ]

    def velocity(comp, row):
        if not beyond(row):
            start = (2 * comp + side) * PZ * 8 + (y_own + row - first_own) % 8
            return ue_ref[pl.ds(start, PZ, stride=8)]
        q = (2 * count + (count - 1) * comp + (row - 1 if side == 0 else row - 6)) * PZ
        return face[q : q + PZ]

    def value_at(src, row):
        r = at(row)
        return advance(
            src[r : r + PZ],
            src[r + 1 : r + 1 + PZ],
            src[r - 1 : r - 1 + PZ],
            src[r + PZ : r + 2 * PZ],
            src[r - PZ : r],
            *[velocity(comp, row) for comp in range(3)],
            lane,
        )

    for row in range(1, total - 1):
        fe[at(row) : at(row) + PZ] = value_at(se, row) * (y_mask if beyond(row) else z_mask)
    for row in range(2, total - 2):
        r = at(row)
        ge[r : r + PZ] = (0.75 * se[r : r + PZ] + 0.25 * value_at(fe, row)) * (y_mask if beyond(row) else z_mask)
    for row in range(3, total - 3):
        r = at(row)
        value = ((1.0 / 3.0) * se[r : r + PZ] + (2.0 / 3.0) * value_at(ge, row))[4 : 4 + CZ]
        if beyond(row):
            joined[pl.ds(40 + row - first_own, CZ, stride=J_ROWS)] = value * inside("gy", side)
        else:
            field_ref[pl.ds(y_own + row - first_own, CZ, stride=CY)] = value


FACE_ROWS = 12 * PZ + 16


LOG2E = 1.4426950408889634


def march(shift_ref, frac_ref, ext_ref, src, start, n, mom_ref, lo):
    quad = ext_ref[0] * (-LOG2E / 1024.0)
    const = ext_ref[1] * (-LOG2E / 1024.0)

    def one(z, state):
        trans, depth, m1, m2, m3 = state
        at = start(z) - shift_ref[z]
        weight = frac_ref[z].astype(F32) * (1.0 / NFRAC)
        near = src[pl.ds(at, n), :]
        far = src[pl.ds(at - 1, n), :]
        g = (1.0 - weight) * near + weight * far
        g2 = g * g
        power = quad * g2 + const
        left = trans * jnp.exp2(power)
        share = trans - left
        s1 = share * g
        s2 = share * g2
        return left, depth + power, m1 + s1, m2 + s2, m3 + s2 * g

    zero = jnp.zeros((n, CX), F32)
    trans, depth, m1, m2, m3 = lax.fori_loop(0, CZ, one, (zero + 1.0, zero, zero, zero, zero), unroll=4)
    for i, value in enumerate((1.0 - trans, m1, m2, m3, depth * (-1.0 / LOG2E))):
        mom_ref[i * CY + lo : i * CY + lo + n] = value


def lower(u_ref, below_ref, above_ref, ss_ref, f1, f2_in, field_in, f2, field_ref):
    for z in (-1, CZ):
        one_plane(f1, z, any_velocity(u_ref, below_ref, above_ref, z), put_second(f2, ss_ref), LOWER_2)
        rows = slice(flat(z), flat(z) + 16)
        f2[rows] = f2[rows] * inside("gz", int(z == CZ))
    run_planes(0, CZ, 4, lambda z: one_plane(f1, z, own_velocity(u_ref, z), put_second(f2, ss_ref), LOWER_2))
    run_planes(0, CZ, 4, lambda z: one_plane(f2, z, own_velocity(u_ref, z), put_field(field_ref, ss_ref), LOWER))


def borders(shift_ref, frac_ref, ext_ref, ss_ref, ue_ref, below_ref, above_ref, field_in,
            field_ref, out_ref, joined, mom_ref, face, se, fe, ge, sem):
    fix_rows(0, ss_ref, ue_ref, below_ref, field_ref, joined, face, se, fe, ge)
    fix_rows(1, ss_ref, ue_ref, above_ref, field_ref, joined, face, se, fe, ge)
    copy = pltpu.make_async_copy(field_ref, out_ref, sem)
    copy.start()
    march(shift_ref, frac_ref, ext_ref, field_ref, lambda z: z * CY + 40, 24, mom_ref, 40)
    for z in range(CZ):
        joined[z * J_ROWS + 40 : z * J_ROWS + 80] = field_ref[z * CY : z * CY + 40]
    copy.wait()


def lights(shift_ref, frac_ref, color_ref, ext_ref, pow_ref, shear_ref, joined_in, mom_in, out_ref, joined, mom_ref, above, turned):
    step = shear_ref[SH_ROWS : SH_ROWS + 16].astype(F32)[0:1]
    index = lax.broadcasted_iota(jnp.int32, (128, CX), 0).astype(F32)
    scale = jnp.sum(jnp.where(index == step, pow_ref[...], 0.0), axis=0, keepdims=True)
    above[...] = shear_ref[0:SH_ROWS].astype(F32) * (scale * (1.0 / 32000.0))
    for z in range(CZ):
        joined[z * J_ROWS + 7 : z * J_ROWS + 37] = above[z * TOP : (z + 1) * TOP]
    march(shift_ref, frac_ref, ext_ref, joined, lambda z: z * J_ROWS + 40, 40, mom_ref, 0)
    moments = [mom_ref[i * CY : (i + 1) * CY] for i in range(5)]
    for c in range(3):
        turned[c * CY : (c + 1) * CY] = (color_ref[c, 0] * moments[0] + color_ref[c, 1] * moments[1]) + (
            color_ref[c, 2] * moments[2] + color_ref[c, 3] * moments[3]
        )
    turned[3 * CY : 4 * CY] = moments[4]
    for h in range(2):
        turned[h * 128 : (h + 1) * 128] = turned[h * 128 : (h + 1) * 128].T
    for d in range(32):
        for h in range(2):
            out_ref[8 * d + 4 * h : 8 * d + 4 * h + 4] = turned[h * 128 + 4 * d : h * 128 + 4 * d + 4]


def finish(rank_ref, got_ref, image_ref, dep, order):
    for k in range(32):
        order[rank_ref[k]] = k
    got = got_ref[...].reshape(32, 8, 128)
    lane = lax.broadcasted_iota(jnp.int32, (32, 8, 128), 2)
    row = lax.broadcasted_iota(jnp.int32, (32, 8, 128), 1)
    depth = jnp.where(lane >= 64, got, pltpu.roll(got, 64, 2))
    depth = jnp.where(row >= 4, depth, pltpu.roll(depth, 4, 1))
    dep[...] = depth.reshape(256, 128)
    run = jnp.zeros((8, 128), F32)
    total = jnp.zeros((8, 128), F32)
    for r in range(32):
        base = pl.multiple_of(order[r] * 8, 8)
        total = total + jnp.exp(-run) * got_ref[pl.ds(base, 8)]
        run = run + dep[pl.ds(base, 8)]
    total = jnp.where((row[0] >= 4) & (lane[0] >= 64), 1.0 - jnp.exp(-run), total)
    for c in range(4):
        h, half = divmod(c, 2)
        image_ref[c] = total[4 * h : 4 * h + 4, 64 * half : 64 * half + 64]


def on_device(scalar, velocity, row_shift, frac_index, brick_rank, color_coeffs, extinction):
    powers = powers_of_two()
    hbm_scalar = pltpu.with_memory_space_constraint(scalar.reshape(CELLS, CX), pltpu.HBM)
    hbm_velocity = pltpu.with_memory_space_constraint(velocity, pltpu.HBM)

    z_face = shaped((12 * CY, CX), BF16)
    z_up, z_down = call(
        pack_z,
        (z_face, z_face),
        [HB, HB],
        [pltpu.VMEM((2, 3 * CY, CX), F32), pltpu.VMEM((2, 3, 2, CY, CX), BF16), pltpu.SemaphoreType.DMA((4,))],
    )(hbm_scalar, hbm_velocity)
    z_below, z_above = shifted(z_up, "gz", 1), shifted(z_down, "gz", -1)

    padded, slab = shaped((SS_ROWS, CX), F32), shaped((CELLS, CX), F32)
    rows, speed = shaped((UE_ROWS, CX), F32), shaped((3, CZ, CY, CX), BF16)
    ss, uv, ue, f1, f2 = call(
        inner, (padded, speed, rows, padded, padded), [HB, HB], [pltpu.SemaphoreType.DMA((8,))], cycles=3000
    )(hbm_scalar, hbm_velocity)

    ss, ue, y_up, y_down = call(
        assemble,
        (padded, rows, shaped((UP_ROWS, CX), BF16), shaped((DOWN_ROWS, CX), BF16)),
        [VM] * 4,
        [pltpu.VMEM((UP_ROWS, CX), F32)],
        {2: 0, 3: 1},
    )(z_below, z_above, ss, ue)
    y_below = shifted(y_up, "gy", 1)
    y_above = shifted(y_down, "gy", -1)

    f1, f2, field, top = call(
        middle,
        (padded, padded, slab, shaped((SH_ROWS + 16, CX), I16)),
        [VM] * 7,
        [pltpu.VMEM((SH_ROWS, CX), F32)],
        {5: 0, 6: 1},
        cycles=2500,
    )(powers, uv, z_below, z_above, ss, f1, f2)
    above = shifted(top, "gy", 1)

    joined_shape, moments_shape = shaped((CZ * J_ROWS, CX), F32), shaped((5 * CY, CX), F32)
    _, field = call(lower, (padded, slab), [VM] * 7, (), {5: 0, 6: 1}, cycles=1000)(
        uv, z_below, z_above, ss, f1, f2, field
    )
    _, field_out, joined, moments = call(
        borders,
        (slab, slab, joined_shape, moments_shape),
        [SM] * 3 + [VM] * 5,
        [pltpu.VMEM((UP_ROWS, CX), F32)] + [pltpu.VMEM((FACE_ROWS, CX), F32)] * 3 + [pltpu.SemaphoreType.DMA],
        {7: 0},
        (VM, HB, VM, VM),
        cycles=2500,
    )(row_shift, frac_index, extinction, ss, ue, y_below, y_above, field)
    sent, _, _ = call(
        lights,
        (shaped((256, CX), F32), joined_shape, moments_shape),
        [SM] * 4 + [VM] * 4,
        [pltpu.VMEM((SH_ROWS, CX), F32), pltpu.VMEM((256, CX), F32)],
        {6: 1, 7: 2},
    )(row_shift, frac_index, color_coeffs, extinction, powers, above, joined, moments)
    got = lax.all_to_all(sent.reshape(32, 8, CX), "gz", split_axis=0, concat_axis=0, tiled=True)

    image = call(
        finish,
        shaped((4, 4, CY), F32),
        [SM, VM],
        [pltpu.VMEM((256, CX), F32), pltpu.SMEM((32,), jnp.int32)],
    )(brick_rank, got.reshape(256, CX))
    return field_out.reshape(CZ, CY, CX), jnp.transpose(image, (0, 2, 1))


def solution(mesh):
    placed = (P("gz", "gy", None), P(None, "gz", "gy", None), P("gz"), P("gz"), P(), P(), P())
    return jax.shard_map(
        on_device,
        mesh=mesh,
        in_specs=placed,
        out_specs=(P("gz", "gy", None), P(None, "gy", "gz")),
        check_vma=False,
    )
```

```python
import jax
import jax.numpy as jnp
import numpy as np
from jax import lax
from jax.experimental import pallas as pl
from jax.experimental.pallas import tpu as pltpu
from jax.sharding import PartitionSpec as P


NFRAC = 8
SHIFT_MAX = 32
CZ, CY, CX = 32, 64, 128
PZ = 40
PLANE = CY
SS_ROWS = PZ * PLANE + 16
CELLS = CZ * CY
VV_PLANE = PZ * PLANE
J_ROWS = 80
UP, DOWN = 6, 3
UP_ROWS, DOWN_ROWS = 1088, 480
TOP = SHIFT_MAX + 1 - 3
SH_ROWS = CZ * TOP
F32, BF16, I16 = jnp.float32, jnp.bfloat16, jnp.int16
VM = pl.BlockSpec(memory_space=pltpu.VMEM)
SM = pl.BlockSpec(memory_space=pltpu.SMEM)
HB = pl.BlockSpec(memory_space=pltpu.HBM)


def call(kernel, outs, ins, scratch=(), aliases=None, out_specs=None, cycles=1000, vmem=16777216):
    return pl.pallas_call(
        kernel,
        out_shape=outs,
        in_specs=list(ins),
        out_specs=out_specs or jax.tree.map(lambda _: VM, outs),
        scratch_shapes=list(scratch),
        input_output_aliases=aliases or {},
        compiler_params=pltpu.CompilerParams(vmem_limit_bytes=vmem),
        cost_estimate=pl.CostEstimate(flops=4096 * cycles, bytes_accessed=1024 * cycles, transcendentals=0),
    )


def shaped(shape, dtype):
    return jax.ShapeDtypeStruct(shape, dtype)


def shifted(value, axis, by):
    count = lax.axis_size(axis)
    return lax.ppermute(value, axis, [(i, (i + by) % count) for i in range(count)])


def chained(value, axis, by):
    count = lax.axis_size(axis)
    return lax.ppermute(value, axis, [(i, i + by) for i in range(count) if 0 <= i + by < count])


def swapped(value, axis, first):
    count = lax.axis_size(axis)
    pairs = [(i, (i + 1) % count) for i in range(first, count, 2)]
    return lax.ppermute(value, axis, pairs + [(b, a) for a, b in pairs])


def split(value):
    high = value.astype(BF16)
    return high, (value - high.astype(F32)).astype(BF16)


def powers_of_two():
    return jnp.asarray(np.repeat((2.0 ** (np.arange(128) - 110.0)).astype(np.float32)[:, None], CX, 1))


def pack_z(s_ref, u_ref, far_ref, near_ref, s_buf, u_buf, sem):
    odd = lax.axis_index("gz") % 2
    copies = []
    for side, top in enumerate((odd, 1 - odd)):
        s_lo = pl.multiple_of(top * (CZ - 3) * CY, CY)
        copies.append(pltpu.make_async_copy(s_ref.at[pl.ds(s_lo, 3 * CY)], s_buf.at[side], sem.at[2 * side]))
        copies.append(pltpu.make_async_copy(u_ref.at[:, pl.ds(top * (CZ - 2), 2)], u_buf.at[side], sem.at[2 * side + 1]))
    for copy in copies:
        copy.start()
    for side, out in enumerate((far_ref, near_ref)):
        copies[2 * side].wait()
        high, low = split(s_buf[side])
        out[0 : 3 * CY] = high
        out[3 * CY : 6 * CY] = low
        copies[2 * side + 1].wait()
        for comp in range(3):
            out[(6 + 2 * comp) * CY : (8 + 2 * comp) * CY] = u_buf[side, comp].reshape(2 * CY, CX)


def flat(z):
    return 8 + PLANE * (z + 4)


def aligned(x):
    return x if isinstance(x, int) else pl.multiple_of(x, 8)


def gain(c, zn, zp, yn, yp, vz, vy, vx, lane):
    xn = jnp.where(lane == CX - 1, 0.0, pltpu.roll(c, CX - 1, 1))
    xp = jnp.where(lane == 0, 0.0, pltpu.roll(c, 1, 1))
    total = (zn + zp) + (yn + yp) + (xn + xp)
    return total - (vz * (zn - zp) + vy * (yn - yp) + vx * (xn - xp))


def first_of(c, g):
    return 0.94 * c + 0.01 * g


def second_of(s, c, g):
    return 0.75 * s + (0.25 * 0.94 * c + 0.25 * 0.01 * g)


def field_of(s, c, g):
    return (1.0 / 3.0) * s + (2.0 / 3.0 * 0.94 * c + 2.0 / 3.0 * 0.01 * g)


FULL = ((0, 16), (16, 16), (32, 16), (48, 16))
UPPER = ((24, 8), (32, 16), (48, 16))
UPPER_2, LOWER_2 = ((16, 16), (32, 16), (48, 16)), ((0, 16),)
EARLY = 30
LOWER = ((0, 16), (16, 8))


def one_plane(src, z, v_of, put, chunks=FULL):
    base = aligned(flat(z))
    near = src.at[pl.ds(aligned(base - 8), CY + 16)]
    after = src.at[pl.ds(aligned(base + PLANE), CY)]
    before = src.at[pl.ds(aligned(base - PLANE), CY)]
    for k, n in chunks:
        lane = lax.broadcasted_iota(jnp.int32, (n, CX), 1)
        c = near[8 + k : 8 + k + n]
        g = gain(
            c,
            after[k : k + n],
            before[k : k + n],
            near[9 + k : 9 + k + n],
            near[7 + k : 7 + k + n],
            *[v_of(comp, k, n) for comp in range(3)],
            lane,
        )
        put(aligned(base + k), k, n, c, g)


def v_at(comp, z):
    return aligned(comp * VV_PLANE + PLANE * (z + 4))


def run_planes(lo, hi, step, body):
    trips = (hi - lo) // step

    def group(i, _):
        for n in range(step):
            body(lo + i * step + n)
        return 0

    lax.fori_loop(0, trips, group, 0)
    for z in range(lo + trips * step, hi):
        body(z)


def speeds(vv_ref, z):
    planes = [vv_ref.at[pl.ds(v_at(comp, z), CY)] for comp in range(3)]
    return lambda comp, k, n: planes[comp][k : k + n]


def put_first(f1):
    def put(at, k, n, c, g):
        f1[pl.ds(at, n)] = first_of(c, g)

    return put


def put_second(f2, ss_ref):
    def put(at, k, n, c, g):
        f2[pl.ds(at, n)] = second_of(ss_ref[pl.ds(at, n)], c, g)

    return put


def put_field(field_ref, ss_ref):
    def put(at, k, n, c, g):
        field_ref[pl.ds(aligned(at - flat(0)), n)] = field_of(ss_ref[pl.ds(at, n)], c, g)

    return put


GROUP = 8


def inner(s_ref, u_ref, ss_ref, vv_ref, f1, f2, uv_ref, sem):
    copies = []
    for c in range(CZ // GROUP):
        rows = GROUP * CY
        copies.append(
            (
                pltpu.make_async_copy(s_ref.at[pl.ds(c * rows, rows)], ss_ref.at[pl.ds(flat(0) + c * rows, rows)], sem.at[2 * c]),
                pltpu.make_async_copy(u_ref.at[:, pl.ds(c * GROUP, GROUP)], uv_ref.at[:, pl.ds(c * GROUP, GROUP)], sem.at[2 * c + 1]),
            )
        )
    for pair in copies:
        for copy in pair:
            copy.start()

    def fresh(z):
        planes = [vv_ref.at[pl.ds(v_at(comp, z), CY)] for comp in range(3)]

        def of(comp, k, n):
            value = 10.0 * uv_ref[comp, z, k : k + n, :].astype(F32)
            planes[comp][k : k + n] = value
            return value

        return of

    for c, pair in enumerate(copies):
        for copy in pair:
            copy.wait()
        lo, hi = max(1, GROUP * c - 1), GROUP * (c + 1) - 1
        run_planes(lo, hi, 4, lambda z: one_plane(ss_ref, z, fresh(z), put_first(f1)))
    for z in (0, CZ - 1):
        of = fresh(z)
        for comp in range(3):
            for k, n in FULL:
                of(comp, k, n)
    run_planes(2, EARLY, 4, lambda z: one_plane(f1, z, speeds(vv_ref, z), put_second(f2, ss_ref), UPPER_2))


def inside(axis, side):
    place = lax.axis_index(axis)
    return jnp.where(place == (lax.axis_size(axis) - 1) * side, 0.0, 1.0)


def assemble(far_ref, near_ref, ss_in, vv_in, ss_ref, vv_ref, up_ref, down_ref, face):
    odd = lax.axis_index("gz") % 2 == 1

    def halo(side, plane, count):
        rows = slice(plane * CY, (plane + count) * CY)
        far, near = far_ref[rows].astype(F32), near_ref[rows].astype(F32)
        return jnp.where(odd, near, far) if side == 0 else jnp.where(odd, far, near)

    for side, z in ((0, -3), (1, CZ)):
        for n in range(3):
            ss_ref[flat(z + n) : flat(z + n) + CY] = (halo(side, n, 1) + halo(side, 3 + n, 1)) * inside("gz", side)
    for side, z in ((0, -2), (1, CZ)):
        for comp in range(3):
            for n in range(2):
                base = v_at(comp, z + n)
                vv_ref[base : base + CY] = 10.0 * halo(side, 6 + 2 * comp + n, 1)
    for out, count, s_lo, v_lo in ((up_ref, UP, CY - UP, CY - UP + 1), (down_ref, DOWN, 0, 0)):
        for row in range(count):
            value = ss_ref[pl.ds(8 + s_lo + row, PZ, stride=PLANE)]
            high = value.astype(BF16).astype(F32)
            face[row * PZ : (row + 1) * PZ] = high
            face[(count + row) * PZ : (count + row + 1) * PZ] = value - high
        for comp in range(3):
            for row in range(count - 1):
                at = 2 * count + (count - 1) * comp + row
                face[at * PZ : (at + 1) * PZ] = 0.1 * vv_ref[pl.ds(comp * VV_PLANE + v_lo + row, PZ, stride=PLANE)]
        out[...] = face[0 : out.shape[0]].astype(BF16)


def middle(pow_ref, vv_ref, ss_ref, f1_in, f2_in, f1, f2, field_ref, shear_ref, top):
    def mask(dst, width):
        for z, side in ((-width, 0), (CZ, 1)):
            rows = slice(flat(z), flat(z) + width * CY)
            dst[rows] = dst[rows] * inside("gz", side)

    for z in (-2, -1, 0, CZ - 1, CZ, CZ + 1):
        one_plane(ss_ref, z, speeds(vv_ref, z), put_first(f1))
    mask(f1, 2)
    for z in (-1, 0, 1, EARLY, EARLY + 1, CZ):
        one_plane(f1, z, speeds(vv_ref, z), put_second(f2, ss_ref), UPPER_2)
    mask(f2, 1)
    run_planes(0, CZ, 4, lambda z: one_plane(f2, z, speeds(vv_ref, z), put_field(field_ref, ss_ref), UPPER))
    for z in range(CZ):
        top[z * TOP : (z + 1) * TOP] = field_ref[z * CY + CY - TOP - 3 : (z + 1) * CY - 3]
    peak = jnp.max(jnp.abs(top[...]), axis=0, keepdims=True)
    enough = pow_ref[...] >= peak
    scale = jnp.min(jnp.where(enough, pow_ref[...], 2.0**17), axis=0, keepdims=True)
    step = jnp.sum(jnp.where(enough, 0.0, 1.0), axis=0, keepdims=True)
    shear_ref[0:SH_ROWS] = jnp.round(top[...] * (32000.0 / scale)).astype(I16)
    shear_ref[SH_ROWS : SH_ROWS + 16] = jnp.broadcast_to(step, (16, CX)).astype(I16)


def fix_rows(side, ss_ref, vv_ref, halo, field_ref, joined, face, se, fe, ge):
    count = (UP, DOWN)[side]
    first_own, first_halo, y_own, total = ((UP, 0, 0, UP + 6), (0, 6, CY - 6, 6 + DOWN))[side]
    lane = lax.broadcasted_iota(jnp.int32, (PZ, CX), 1)
    spot = lax.broadcasted_iota(jnp.int32, (PZ, CX), 0)
    z_mask = jnp.where(spot < 4, inside("gz", 0), jnp.where(spot >= 4 + CZ, inside("gz", 1), 1.0))
    y_mask = z_mask * inside("gy", side)
    face[0 : halo.shape[0]] = halo[...].astype(F32)

    def at(row):
        return 8 + row * PZ

    def beyond(row):
        return not first_own <= row < first_own + 6

    for n in range(6):
        r = at(first_own + n)
        se[r : r + PZ] = ss_ref[pl.ds(8 + y_own + n, PZ, stride=PLANE)]
    for n in range(count):
        r = at(first_halo + n)
        value = face[n * PZ : (n + 1) * PZ] + face[(count + n) * PZ : (count + n + 1) * PZ]
        se[r : r + PZ] = value * inside("gy", side)

    def velocity(comp, row):
        if not beyond(row):
            return vv_ref[pl.ds(comp * VV_PLANE + y_own + row - first_own, PZ, stride=PLANE)]
        q = (2 * count + (count - 1) * comp + (row - 1 if side == 0 else row - 6)) * PZ
        return 10.0 * face[q : q + PZ]

    def stage(src, row, of, *base):
        r = at(row)
        c = src[r : r + PZ]
        g = gain(
            c,
            src[r + 1 : r + 1 + PZ],
            src[r - 1 : r - 1 + PZ],
            src[r + PZ : r + 2 * PZ],
            src[r - PZ : r],
            *[velocity(comp, row) for comp in range(3)],
            lane,
        )
        return of(*[b[r : r + PZ] for b in base], c, g)

    for row in range(1, total - 1):
        fe[at(row) : at(row) + PZ] = stage(se, row, first_of) * (y_mask if beyond(row) else z_mask)
    for row in range(2, total - 2):
        ge[at(row) : at(row) + PZ] = stage(fe, row, second_of, se) * (y_mask if beyond(row) else z_mask)
    for row in range(3, total - 3):
        value = stage(ge, row, field_of, se)[4 : 4 + CZ]
        if beyond(row):
            joined[pl.ds(40 + row - first_own, CZ, stride=J_ROWS)] = value * inside("gy", side)
        else:
            field_ref[pl.ds(y_own + row - first_own, CZ, stride=CY)] = value


FACE_ROWS = 12 * PZ + 16


LOG2E = 1.4426950408889634


def march(shift_ref, frac_ref, ext_ref, src, start, n, mom_ref, lo):
    quad = ext_ref[0] * (-LOG2E / 1024.0)
    const = ext_ref[1] * (-LOG2E / 1024.0)

    def one(z, state):
        trans, depth, m1, m2, m3 = state
        at = start(z) - shift_ref[z]
        weight = frac_ref[z].astype(F32) * (1.0 / NFRAC)
        near = src[pl.ds(at, n), :]
        far = src[pl.ds(at - 1, n), :]
        g = (1.0 - weight) * near + weight * far
        g2 = g * g
        power = quad * g2 + const
        left = trans * jnp.exp2(power)
        share = trans - left
        s1 = share * g
        s2 = share * g2
        return left, depth + power, m1 + s1, m2 + s2, m3 + s2 * g

    zero = jnp.zeros((n, CX), F32)
    trans, depth, m1, m2, m3 = lax.fori_loop(0, CZ, one, (zero + 1.0, zero, zero, zero, zero), unroll=4)
    for i, value in enumerate((1.0 - trans, m1, m2, m3, depth * (-1.0 / LOG2E))):
        mom_ref[i * CY + lo : i * CY + lo + n] = value


def lower(vv_ref, ss_ref, f1, f2_in, field_in, f2, field_ref):
    for z in (-1, CZ):
        one_plane(f1, z, speeds(vv_ref, z), put_second(f2, ss_ref), LOWER_2)
        rows = slice(flat(z), flat(z) + 16)
        f2[rows] = f2[rows] * inside("gz", int(z == CZ))
    run_planes(0, CZ, 8, lambda z: one_plane(f1, z, speeds(vv_ref, z), put_second(f2, ss_ref), LOWER_2))
    run_planes(0, CZ, 8, lambda z: one_plane(f2, z, speeds(vv_ref, z), put_field(field_ref, ss_ref), LOWER))


def borders(shift_ref, frac_ref, ext_ref, ss_ref, vv_ref, below_ref, above_ref, field_in,
            field_ref, joined, mom_ref, face, se, fe, ge):
    fix_rows(0, ss_ref, vv_ref, below_ref, field_ref, joined, face, se, fe, ge)
    fix_rows(1, ss_ref, vv_ref, above_ref, field_ref, joined, face, se, fe, ge)
    march(shift_ref, frac_ref, ext_ref, field_ref, lambda z: z * CY + 40, 24, mom_ref, 40)
    for z in range(CZ):
        joined[z * J_ROWS + 40 : z * J_ROWS + 80] = field_ref[z * CY : z * CY + 40]


def lights(shift_ref, frac_ref, color_ref, ext_ref, pow_ref, shear_ref, field_ref, joined_in, mom_in,
           out_ref, joined, mom_ref, field_out_ref, above, turned, sem):
    copy = pltpu.make_async_copy(field_ref, field_out_ref, sem)
    copy.start()
    step = shear_ref[SH_ROWS : SH_ROWS + 16].astype(F32)[0:1]
    index = lax.broadcasted_iota(jnp.int32, (128, CX), 0).astype(F32)
    scale = jnp.sum(jnp.where(index == step, pow_ref[...], 0.0), axis=0, keepdims=True)
    above[...] = shear_ref[0:SH_ROWS].astype(F32) * (scale * (inside("gy", 0) * (1.0 / 32000.0)))
    for z in range(CZ):
        joined[z * J_ROWS + 7 : z * J_ROWS + 37] = above[z * TOP : (z + 1) * TOP]
    march(shift_ref, frac_ref, ext_ref, joined, lambda z: z * J_ROWS + 40, 40, mom_ref, 0)
    moments = [mom_ref[i * CY : (i + 1) * CY] for i in range(5)]
    for c in range(3):
        turned[c * CY : (c + 1) * CY] = (color_ref[c, 0] * moments[0] + color_ref[c, 1] * moments[1]) + (
            color_ref[c, 2] * moments[2] + color_ref[c, 3] * moments[3]
        )
    turned[3 * CY : 4 * CY] = moments[4]
    for h in range(2):
        turned[h * 128 : (h + 1) * 128] = turned[h * 128 : (h + 1) * 128].T
    for d in range(32):
        for h in range(2):
            out_ref[8 * d + 4 * h : 8 * d + 4 * h + 4] = turned[h * 128 + 4 * d : h * 128 + 4 * d + 4]
    copy.wait()


def finish(rank_ref, got_ref, image_ref, dep, order):
    for k in range(32):
        order[rank_ref[k]] = k
    got = got_ref[...].reshape(32, 8, 128)
    lane = lax.broadcasted_iota(jnp.int32, (32, 8, 128), 2)
    row = lax.broadcasted_iota(jnp.int32, (32, 8, 128), 1)
    depth = jnp.where(lane >= 64, got, pltpu.roll(got, 64, 2))
    depth = jnp.where(row >= 4, depth, pltpu.roll(depth, 4, 1))
    dep[...] = depth.reshape(256, 128)
    run = jnp.zeros((8, 128), F32)
    total = jnp.zeros((8, 128), F32)
    for r in range(32):
        base = pl.multiple_of(order[r] * 8, 8)
        total = total + jnp.exp(-run) * got_ref[pl.ds(base, 8)]
        run = run + dep[pl.ds(base, 8)]
    total = jnp.where((row[0] >= 4) & (lane[0] >= 64), 1.0 - jnp.exp(-run), total)
    for c in range(4):
        h, half = divmod(c, 2)
        image_ref[c] = total[4 * h : 4 * h + 4, 64 * half : 64 * half + 64]


def on_device(scalar, velocity, row_shift, frac_index, brick_rank, color_coeffs, extinction):
    powers = powers_of_two()
    hbm_scalar = pltpu.with_memory_space_constraint(scalar.reshape(CELLS, CX), pltpu.HBM)
    hbm_velocity = pltpu.with_memory_space_constraint(velocity, pltpu.HBM)

    z_face = shaped((12 * CY, CX), BF16)
    to_far, to_near = call(
        pack_z,
        (z_face, z_face),
        [HB, HB],
        [pltpu.VMEM((2, 3 * CY, CX), F32), pltpu.VMEM((2, 3, 2, CY, CX), BF16), pltpu.SemaphoreType.DMA((4,))],
    )(hbm_scalar, hbm_velocity)
    far = swapped(to_far, "gz", 1)
    near = swapped(to_near, "gz", 0)

    padded, slab = shaped((SS_ROWS, CX), F32), shaped((CELLS, CX), F32)
    speed = shaped((3 * VV_PLANE, CX), F32)
    ss, vv, f1, f2 = call(
        inner,
        (padded, speed, padded, padded),
        [HB, HB],
        [pltpu.VMEM((3, CZ, CY, CX), BF16), pltpu.SemaphoreType.DMA((8,))],
        cycles=3000,
    )(hbm_scalar, hbm_velocity)

    ss, vv, y_up, y_down = call(
        assemble,
        (padded, speed, shaped((UP_ROWS, CX), BF16), shaped((DOWN_ROWS, CX), BF16)),
        [VM] * 4,
        [pltpu.VMEM((UP_ROWS, CX), F32)],
        {2: 0, 3: 1},
    )(far, near, ss, vv)
    y_below = shifted(y_up, "gy", 1)
    y_above = shifted(y_down, "gy", -1)

    f1, f2, field, top = call(
        middle,
        (padded, padded, slab, shaped((SH_ROWS + 16, CX), I16)),
        [VM] * 5,
        [pltpu.VMEM((SH_ROWS, CX), F32)],
        {3: 0, 4: 1},
        cycles=2500,
    )(powers, vv, ss, f1, f2)
    above = chained(top, "gy", 1)

    joined_shape, moments_shape = shaped((CZ * J_ROWS, CX), F32), shaped((5 * CY, CX), F32)
    _, field = call(lower, (padded, slab), [VM] * 5, (), {3: 0, 4: 1}, cycles=1000)(vv, ss, f1, f2, field)
    field, joined, moments = call(
        borders,
        (slab, joined_shape, moments_shape),
        [SM] * 3 + [VM] * 5,
        [pltpu.VMEM((UP_ROWS, CX), F32)] + [pltpu.VMEM((FACE_ROWS, CX), F32)] * 3,
        {7: 0},
        cycles=2500,
    )(row_shift, frac_index, extinction, ss, vv, y_below, y_above, field)
    sent, _, _, field_out = call(
        lights,
        (shaped((256, CX), F32), joined_shape, moments_shape, slab),
        [SM] * 4 + [VM] * 5,
        [pltpu.VMEM((SH_ROWS, CX), F32), pltpu.VMEM((256, CX), F32), pltpu.SemaphoreType.DMA],
        {7: 1, 8: 2},
        (VM, VM, VM, HB),
    )(row_shift, frac_index, color_coeffs, extinction, powers, above, field, joined, moments)
    got = lax.all_to_all(sent.reshape(32, 8, CX), "gz", split_axis=0, concat_axis=0, tiled=True)

    image = call(
        finish,
        shaped((4, 4, CY), F32),
        [SM, VM],
        [pltpu.VMEM((256, CX), F32), pltpu.SMEM((32,), jnp.int32)],
    )(brick_rank, got.reshape(256, CX))
    return field_out.reshape(CZ, CY, CX), jnp.transpose(image, (0, 2, 1))


def solution(mesh):
    placed = (P("gz", "gy", None), P(None, "gz", "gy", None), P("gz"), P("gz"), P(), P(), P())
    return jax.shard_map(
        on_device,
        mesh=mesh,
        in_specs=placed,
        out_specs=(P("gz", "gy", None), P(None, "gy", "gz")),
        check_vma=False,
    )
```

```python
import jax
import jax.numpy as jnp
import numpy as np
from jax import lax
from jax.experimental import pallas as pl
from jax.experimental.pallas import tpu as pltpu
from jax.sharding import PartitionSpec as P


NFRAC = 8
SHIFT_MAX = 32
CZ, CY, CX = 32, 64, 128
PZ = 40
PLANE = CY
SS_ROWS = PZ * PLANE + 16
CELLS = CZ * CY
VV_PLANE = PZ * PLANE
J_ROWS = 80
UP, DOWN = 6, 3
LOW = 3
UP_ROWS, DOWN_ROWS = (UP + LOW + 15) * PZ, (DOWN + LOW + 6) * PZ
TOP = SHIFT_MAX + 1 - 3
SH_ROWS = CZ * TOP
F32, BF16, I16 = jnp.float32, jnp.bfloat16, jnp.int16
VM = pl.BlockSpec(memory_space=pltpu.VMEM)
SM = pl.BlockSpec(memory_space=pltpu.SMEM)
HB = pl.BlockSpec(memory_space=pltpu.HBM)


def call(kernel, outs, ins, scratch=(), aliases=None, out_specs=None, cycles=1000, vmem=16777216):
    return pl.pallas_call(
        kernel,
        out_shape=outs,
        in_specs=list(ins),
        out_specs=out_specs or jax.tree.map(lambda _: VM, outs),
        scratch_shapes=list(scratch),
        input_output_aliases=aliases or {},
        compiler_params=pltpu.CompilerParams(vmem_limit_bytes=vmem),
        cost_estimate=pl.CostEstimate(flops=4096 * cycles, bytes_accessed=1024 * cycles, transcendentals=0),
    )


def shaped(shape, dtype):
    return jax.ShapeDtypeStruct(shape, dtype)


def shifted(value, axis, by):
    count = lax.axis_size(axis)
    return lax.ppermute(value, axis, [(i, (i + by) % count) for i in range(count)])


def chained(value, axis, by):
    count = lax.axis_size(axis)
    return lax.ppermute(value, axis, [(i, i + by) for i in range(count) if 0 <= i + by < count])


def swapped(value, axis, first):
    count = lax.axis_size(axis)
    pairs = [(i, (i + 1) % count) for i in range(first, count, 2)]
    return lax.ppermute(value, axis, pairs + [(b, a) for a, b in pairs])


def split(value):
    high = value.astype(BF16)
    return high, (value - high.astype(F32)).astype(BF16)


def powers_of_two():
    return jnp.asarray(np.repeat((2.0 ** (np.arange(128) - 110.0)).astype(np.float32)[:, None], CX, 1))


def pack_z(s_ref, u_ref, far_ref, near_ref, s_buf, u_buf, sem):
    odd = lax.axis_index("gz") % 2
    copies = []
    for side, top in enumerate((odd, 1 - odd)):
        s_lo = pl.multiple_of(top * (CZ - 3) * CY, CY)
        copies.append(pltpu.make_async_copy(s_ref.at[pl.ds(s_lo, 3 * CY)], s_buf.at[side], sem.at[2 * side]))
        copies.append(pltpu.make_async_copy(u_ref.at[:, pl.ds(top * (CZ - 2), 2)], u_buf.at[side], sem.at[2 * side + 1]))
    for copy in copies:
        copy.start()
    for side, out in enumerate((far_ref, near_ref)):
        copies[2 * side].wait()
        high, low = split(s_buf[side])
        out[0 : 3 * CY] = high
        out[3 * CY : 6 * CY] = low
        copies[2 * side + 1].wait()
        for comp in range(3):
            out[(6 + 2 * comp) * CY : (8 + 2 * comp) * CY] = u_buf[side, comp].reshape(2 * CY, CX)


def flat(z):
    return 8 + PLANE * (z + 4)


def aligned(x):
    return x if isinstance(x, int) else pl.multiple_of(x, 8)


def gain(c, zn, zp, yn, yp, vz, vy, vx, lane):
    xn = jnp.where(lane == CX - 1, 0.0, pltpu.roll(c, CX - 1, 1))
    xp = jnp.where(lane == 0, 0.0, pltpu.roll(c, 1, 1))
    total = (zn + zp) + (yn + yp) + (xn + xp)
    return total - (vz * (zn - zp) + vy * (yn - yp) + vx * (xn - xp))


def first_of(c, g):
    return 0.94 * c + 0.01 * g


def second_of(s, c, g):
    return 0.75 * s + (0.25 * 0.94 * c + 0.25 * 0.01 * g)


def field_of(s, c, g):
    return (1.0 / 3.0) * s + (2.0 / 3.0 * 0.94 * c + 2.0 / 3.0 * 0.01 * g)


FULL = ((0, 16), (16, 16), (32, 16), (48, 16))
UPPER = ((24, 8), (32, 16), (48, 16))
UPPER_2, LOWER_2 = ((16, 16), (32, 16), (48, 16)), ((0, 16),)
EARLY = 30
LOWER = ((0, 16), (16, 8))


def one_plane(src, z, v_of, put, chunks=FULL):
    base = aligned(flat(z))
    near = src.at[pl.ds(aligned(base - 8), CY + 16)]
    after = src.at[pl.ds(aligned(base + PLANE), CY)]
    before = src.at[pl.ds(aligned(base - PLANE), CY)]
    for k, n in chunks:
        lane = lax.broadcasted_iota(jnp.int32, (n, CX), 1)
        c = near[8 + k : 8 + k + n]
        g = gain(
            c,
            after[k : k + n],
            before[k : k + n],
            near[9 + k : 9 + k + n],
            near[7 + k : 7 + k + n],
            *[v_of(comp, k, n) for comp in range(3)],
            lane,
        )
        put(aligned(base + k), k, n, c, g)


def v_at(comp, z):
    return aligned(comp * VV_PLANE + PLANE * (z + 4))


def run_planes(lo, hi, step, body):
    trips = (hi - lo) // step

    def group(i, _):
        for n in range(step):
            body(lo + i * step + n)
        return 0

    lax.fori_loop(0, trips, group, 0)
    for z in range(lo + trips * step, hi):
        body(z)


def speeds(vv_ref, z):
    planes = [vv_ref.at[pl.ds(v_at(comp, z), CY)] for comp in range(3)]
    return lambda comp, k, n: planes[comp][k : k + n]


def put_first(f1):
    def put(at, k, n, c, g):
        f1[pl.ds(at, n)] = first_of(c, g)

    return put


def put_second(f2, ss_ref):
    def put(at, k, n, c, g):
        f2[pl.ds(at, n)] = second_of(ss_ref[pl.ds(at, n)], c, g)

    return put


def put_field(field_ref, ss_ref):
    def put(at, k, n, c, g):
        field_ref[pl.ds(aligned(at - flat(0)), n)] = field_of(ss_ref[pl.ds(at, n)], c, g)

    return put


GROUP = 8


def inner(s_ref, u_ref, ss_ref, vv_ref, f1, f2, uv_ref, sem):
    copies = []
    for c in range(CZ // GROUP):
        rows = GROUP * CY
        copies.append(
            (
                pltpu.make_async_copy(s_ref.at[pl.ds(c * rows, rows)], ss_ref.at[pl.ds(flat(0) + c * rows, rows)], sem.at[2 * c]),
                pltpu.make_async_copy(u_ref.at[:, pl.ds(c * GROUP, GROUP)], uv_ref.at[:, pl.ds(c * GROUP, GROUP)], sem.at[2 * c + 1]),
            )
        )
    for pair in copies:
        for copy in pair:
            copy.start()

    def fresh(z):
        planes = [vv_ref.at[pl.ds(v_at(comp, z), CY)] for comp in range(3)]

        def of(comp, k, n):
            value = 10.0 * uv_ref[comp, z, k : k + n, :].astype(F32)
            planes[comp][k : k + n] = value
            return value

        return of

    for c, pair in enumerate(copies):
        for copy in pair:
            copy.wait()
        lo, hi = max(1, GROUP * c - 1), GROUP * (c + 1) - 1
        run_planes(lo, hi, 4, lambda z: one_plane(ss_ref, z, fresh(z), put_first(f1)))
    for z in (0, CZ - 1):
        of = fresh(z)
        for comp in range(3):
            for k, n in FULL:
                of(comp, k, n)
    run_planes(2, EARLY, 4, lambda z: one_plane(f1, z, speeds(vv_ref, z), put_second(f2, ss_ref), UPPER_2))


def inside(axis, side):
    place = lax.axis_index(axis)
    return jnp.where(place == (lax.axis_size(axis) - 1) * side, 0.0, 1.0)


def assemble(far_ref, near_ref, ss_in, vv_in, ss_ref, vv_ref, up_ref, down_ref, face):
    odd = lax.axis_index("gz") % 2 == 1

    def halo(side, plane, count):
        rows = slice(plane * CY, (plane + count) * CY)
        far, near = far_ref[rows].astype(F32), near_ref[rows].astype(F32)
        return jnp.where(odd, near, far) if side == 0 else jnp.where(odd, far, near)

    for side, z in ((0, -3), (1, CZ)):
        for n in range(3):
            ss_ref[flat(z + n) : flat(z + n) + CY] = (halo(side, n, 1) + halo(side, 3 + n, 1)) * inside("gz", side)
    for side, z in ((0, -2), (1, CZ)):
        for comp in range(3):
            for n in range(2):
                base = v_at(comp, z + n)
                vv_ref[base : base + CY] = 10.0 * halo(side, 6 + 2 * comp + n, 1)
    for out, count, s_lo, v_lo in ((up_ref, UP, CY - UP, CY - UP + 1), (down_ref, DOWN, 0, 0)):
        for row in range(count):
            value = ss_ref[pl.ds(8 + s_lo + row, PZ, stride=PLANE)]
            high = value.astype(BF16).astype(F32)
            face[row * PZ : (row + 1) * PZ] = high
            at = LOW + row
            if at >= count:
                face[at * PZ : (at + 1) * PZ] = value - high
        for comp in range(3):
            for row in range(count - 1):
                at = count + LOW + (count - 1) * comp + row
                face[at * PZ : (at + 1) * PZ] = 0.1 * vv_ref[pl.ds(comp * VV_PLANE + v_lo + row, PZ, stride=PLANE)]
        out[...] = face[0 : out.shape[0]].astype(BF16)


def middle(pow_ref, vv_ref, ss_ref, f1_in, f2_in, f1, f2, field_ref, shear_ref, top):
    def mask(dst, width):
        for z, side in ((-width, 0), (CZ, 1)):
            rows = slice(flat(z), flat(z) + width * CY)
            dst[rows] = dst[rows] * inside("gz", side)

    for z in (-2, -1, 0, CZ - 1, CZ, CZ + 1):
        one_plane(ss_ref, z, speeds(vv_ref, z), put_first(f1))
    mask(f1, 2)
    for z in (-1, 0, 1, EARLY, EARLY + 1, CZ):
        one_plane(f1, z, speeds(vv_ref, z), put_second(f2, ss_ref), UPPER_2)
    mask(f2, 1)
    run_planes(0, CZ, 4, lambda z: one_plane(f2, z, speeds(vv_ref, z), put_field(field_ref, ss_ref), UPPER))
    for z in range(CZ):
        top[z * TOP : (z + 1) * TOP] = field_ref[z * CY + CY - TOP - 3 : (z + 1) * CY - 3]
    peak = jnp.max(jnp.abs(top[...]), axis=0, keepdims=True)
    enough = pow_ref[...] >= peak
    scale = jnp.min(jnp.where(enough, pow_ref[...], 2.0**17), axis=0, keepdims=True)
    step = jnp.sum(jnp.where(enough, 0.0, 1.0), axis=0, keepdims=True)
    shear_ref[0:SH_ROWS] = jnp.round(top[...] * (32000.0 / scale)).astype(I16)
    shear_ref[SH_ROWS : SH_ROWS + 16] = jnp.broadcast_to(step, (16, CX)).astype(I16)


def fix_rows(side, ss_ref, vv_ref, halo, field_ref, joined, face, se, fe, ge):
    count = (UP, DOWN)[side]
    first_own, first_halo, y_own, total = ((UP, 0, 0, UP + 6), (0, 6, CY - 6, 6 + DOWN))[side]
    lane = lax.broadcasted_iota(jnp.int32, (PZ, CX), 1)
    spot = lax.broadcasted_iota(jnp.int32, (PZ, CX), 0)
    z_mask = jnp.where(spot < 4, inside("gz", 0), jnp.where(spot >= 4 + CZ, inside("gz", 1), 1.0))
    y_mask = z_mask * inside("gy", side)
    face[0 : halo.shape[0]] = halo[...].astype(F32)

    def at(row):
        return 8 + row * PZ

    def beyond(row):
        return not first_own <= row < first_own + 6

    for n in range(6):
        r = at(first_own + n)
        se[r : r + PZ] = ss_ref[pl.ds(8 + y_own + n, PZ, stride=PLANE)]
    for n in range(count):
        r = at(first_halo + n)
        value = face[n * PZ : (n + 1) * PZ]
        if n >= count - LOW:
            value = value + face[(LOW + n) * PZ : (LOW + n + 1) * PZ]
        se[r : r + PZ] = value * inside("gy", side)

    def velocity(comp, row):
        if not beyond(row):
            return vv_ref[pl.ds(comp * VV_PLANE + y_own + row - first_own, PZ, stride=PLANE)]
        q = (count + LOW + (count - 1) * comp + (row - 1 if side == 0 else row - 6)) * PZ
        return 10.0 * face[q : q + PZ]

    def stage(src, row, of, *base):
        r = at(row)
        c = src[r : r + PZ]
        g = gain(
            c,
            src[r + 1 : r + 1 + PZ],
            src[r - 1 : r - 1 + PZ],
            src[r + PZ : r + 2 * PZ],
            src[r - PZ : r],
            *[velocity(comp, row) for comp in range(3)],
            lane,
        )
        return of(*[b[r : r + PZ] for b in base], c, g)

    for row in range(1, total - 1):
        fe[at(row) : at(row) + PZ] = stage(se, row, first_of) * (y_mask if beyond(row) else z_mask)
    for row in range(2, total - 2):
        ge[at(row) : at(row) + PZ] = stage(fe, row, second_of, se) * (y_mask if beyond(row) else z_mask)
    for row in range(3, total - 3):
        value = stage(ge, row, field_of, se)[4 : 4 + CZ]
        if beyond(row):
            joined[pl.ds(40 + row - first_own, CZ, stride=J_ROWS)] = value * inside("gy", side)
        else:
            field_ref[pl.ds(y_own + row - first_own, CZ, stride=CY)] = value


FACE_ROWS = 12 * PZ + 16


LOG2E = 1.4426950408889634


def march(shift_ref, frac_ref, ext_ref, src, start, n, mom_ref, lo):
    quad = ext_ref[0] * (-LOG2E / 1024.0)
    const = ext_ref[1] * (-LOG2E / 1024.0)

    def one(z, state):
        trans, depth, m1, m2, m3 = state
        at = start(z) - shift_ref[z]
        weight = frac_ref[z].astype(F32) * (1.0 / NFRAC)
        near = src[pl.ds(at, n), :]
        far = src[pl.ds(at - 1, n), :]
        g = (1.0 - weight) * near + weight * far
        g2 = g * g
        power = quad * g2 + const
        left = trans * jnp.exp2(power)
        share = trans - left
        s1 = share * g
        s2 = share * g2
        return left, depth + power, m1 + s1, m2 + s2, m3 + s2 * g

    zero = jnp.zeros((n, CX), F32)
    trans, depth, m1, m2, m3 = lax.fori_loop(0, CZ, one, (zero + 1.0, zero, zero, zero, zero), unroll=4)
    for i, value in enumerate((1.0 - trans, m1, m2, m3, depth * (-1.0 / LOG2E))):
        mom_ref[i * CY + lo : i * CY + lo + n] = value


def lower(vv_ref, ss_ref, f1, f2_in, field_in, f2, field_ref):
    for z in (-1, CZ):
        one_plane(f1, z, speeds(vv_ref, z), put_second(f2, ss_ref), LOWER_2)
        rows = slice(flat(z), flat(z) + 16)
        f2[rows] = f2[rows] * inside("gz", int(z == CZ))
    run_planes(0, CZ, 8, lambda z: one_plane(f1, z, speeds(vv_ref, z), put_second(f2, ss_ref), LOWER_2))
    run_planes(0, CZ, 8, lambda z: one_plane(f2, z, speeds(vv_ref, z), put_field(field_ref, ss_ref), LOWER))


def high_rows(shift_ref, frac_ref, ext_ref, ss_ref, vv_ref, above_ref, field_in, field_ref, mom_ref, face, se, fe, ge):
    fix_rows(1, ss_ref, vv_ref, above_ref, field_ref, None, face, se, fe, ge)
    march(shift_ref, frac_ref, ext_ref, field_ref, lambda z: z * CY + 40, 24, mom_ref, 40)


def low_rows(ss_ref, vv_ref, below_ref, field_in, field_ref, joined, face, se, fe, ge):
    fix_rows(0, ss_ref, vv_ref, below_ref, field_ref, joined, face, se, fe, ge)
    for z in range(CZ):
        joined[z * J_ROWS + 40 : z * J_ROWS + 80] = field_ref[z * CY : z * CY + 40]


def lights(shift_ref, frac_ref, color_ref, ext_ref, pow_ref, shear_ref, field_ref, joined_in, mom_in,
           out_ref, joined, mom_ref, field_out_ref, above, turned, sem):
    copy = pltpu.make_async_copy(field_ref, field_out_ref, sem)
    copy.start()
    step = shear_ref[SH_ROWS : SH_ROWS + 16].astype(F32)[0:1]
    index = lax.broadcasted_iota(jnp.int32, (128, CX), 0).astype(F32)
    scale = jnp.sum(jnp.where(index == step, pow_ref[...], 0.0), axis=0, keepdims=True)
    above[...] = shear_ref[0:SH_ROWS].astype(F32) * (scale * (inside("gy", 0) * (1.0 / 32000.0)))
    for z in range(CZ):
        joined[z * J_ROWS + 7 : z * J_ROWS + 37] = above[z * TOP : (z + 1) * TOP]
    march(shift_ref, frac_ref, ext_ref, joined, lambda z: z * J_ROWS + 40, 40, mom_ref, 0)
    moments = [mom_ref[i * CY : (i + 1) * CY] for i in range(5)]
    for c in range(3):
        turned[c * CY : (c + 1) * CY] = (color_ref[c, 0] * moments[0] + color_ref[c, 1] * moments[1]) + (
            color_ref[c, 2] * moments[2] + color_ref[c, 3] * moments[3]
        )
    turned[3 * CY : 4 * CY] = moments[4]
    for h in range(2):
        turned[h * 128 : (h + 1) * 128] = turned[h * 128 : (h + 1) * 128].T
    for d in range(32):
        for h in range(2):
            out_ref[8 * d + 4 * h : 8 * d + 4 * h + 4] = turned[h * 128 + 4 * d : h * 128 + 4 * d + 4]
    copy.wait()


def finish(rank_ref, got_ref, image_ref, dep, order):
    for k in range(32):
        order[rank_ref[k]] = k
    got = got_ref[...].reshape(32, 8, 128)
    lane = lax.broadcasted_iota(jnp.int32, (32, 8, 128), 2)
    row = lax.broadcasted_iota(jnp.int32, (32, 8, 128), 1)
    depth = jnp.where(lane >= 64, got, pltpu.roll(got, 64, 2))
    depth = jnp.where(row >= 4, depth, pltpu.roll(depth, 4, 1))
    dep[...] = depth.reshape(256, 128)
    run = jnp.zeros((8, 128), F32)
    total = jnp.zeros((8, 128), F32)
    for r in range(32):
        base = pl.multiple_of(order[r] * 8, 8)
        total = total + jnp.exp(-run) * got_ref[pl.ds(base, 8)]
        run = run + dep[pl.ds(base, 8)]
    total = jnp.where((row[0] >= 4) & (lane[0] >= 64), 1.0 - jnp.exp(-run), total)
    for c in range(4):
        h, half = divmod(c, 2)
        image_ref[c] = total[4 * h : 4 * h + 4, 64 * half : 64 * half + 64]


def on_device(scalar, velocity, row_shift, frac_index, brick_rank, color_coeffs, extinction):
    powers = powers_of_two()
    hbm_scalar = pltpu.with_memory_space_constraint(scalar.reshape(CELLS, CX), pltpu.HBM)
    hbm_velocity = pltpu.with_memory_space_constraint(velocity, pltpu.HBM)

    z_face = shaped((12 * CY, CX), BF16)
    to_far, to_near = call(
        pack_z,
        (z_face, z_face),
        [HB, HB],
        [pltpu.VMEM((2, 3 * CY, CX), F32), pltpu.VMEM((2, 3, 2, CY, CX), BF16), pltpu.SemaphoreType.DMA((4,))],
    )(hbm_scalar, hbm_velocity)
    far = swapped(to_far, "gz", 1)
    near = swapped(to_near, "gz", 0)

    padded, slab = shaped((SS_ROWS, CX), F32), shaped((CELLS, CX), F32)
    speed = shaped((3 * VV_PLANE, CX), F32)
    ss, vv, f1, f2 = call(
        inner,
        (padded, speed, padded, padded),
        [HB, HB],
        [pltpu.VMEM((3, CZ, CY, CX), BF16), pltpu.SemaphoreType.DMA((8,))],
        cycles=3000,
    )(hbm_scalar, hbm_velocity)

    ss, vv, y_up, y_down = call(
        assemble,
        (padded, speed, shaped((UP_ROWS, CX), BF16), shaped((DOWN_ROWS, CX), BF16)),
        [VM] * 4,
        [pltpu.VMEM((UP_ROWS, CX), F32)],
        {2: 0, 3: 1},
    )(far, near, ss, vv)
    y_below = shifted(y_up, "gy", 1)
    y_above = shifted(y_down, "gy", -1)

    f1, f2, field, top = call(
        middle,
        (padded, padded, slab, shaped((SH_ROWS + 16, CX), I16)),
        [VM] * 5,
        [pltpu.VMEM((SH_ROWS, CX), F32)],
        {3: 0, 4: 1},
        cycles=2500,
    )(powers, vv, ss, f1, f2)
    above = chained(top, "gy", 1)

    joined_shape, moments_shape = shaped((CZ * J_ROWS, CX), F32), shaped((5 * CY, CX), F32)
    _, field = call(lower, (padded, slab), [VM] * 5, (), {3: 0, 4: 1}, cycles=1000)(vv, ss, f1, f2, field)
    scratch = [pltpu.VMEM((UP_ROWS, CX), F32)] + [pltpu.VMEM((FACE_ROWS, CX), F32)] * 3
    field, moments = call(
        high_rows, (slab, moments_shape), [SM] * 3 + [VM] * 4, scratch, {6: 0}, cycles=1500
    )(row_shift, frac_index, extinction, ss, vv, y_above, field)
    field, joined = call(low_rows, (slab, joined_shape), [VM] * 4, scratch, {3: 0}, cycles=1500)(
        ss, vv, y_below, field
    )
    sent, _, _, field_out = call(
        lights,
        (shaped((256, CX), F32), joined_shape, moments_shape, slab),
        [SM] * 4 + [VM] * 5,
        [pltpu.VMEM((SH_ROWS, CX), F32), pltpu.VMEM((256, CX), F32), pltpu.SemaphoreType.DMA],
        {7: 1, 8: 2},
        (VM, VM, VM, HB),
    )(row_shift, frac_index, color_coeffs, extinction, powers, above, field, joined, moments)
    got = lax.all_to_all(sent.reshape(32, 8, CX), "gz", split_axis=0, concat_axis=0, tiled=True)

    image = call(
        finish,
        shaped((4, 4, CY), F32),
        [SM, VM],
        [pltpu.VMEM((256, CX), F32), pltpu.SMEM((32,), jnp.int32)],
    )(brick_rank, got.reshape(256, CX))
    return field_out.reshape(CZ, CY, CX), jnp.transpose(image, (0, 2, 1))


def solution(mesh):
    placed = (P("gz", "gy", None), P(None, "gz", "gy", None), P("gz"), P("gz"), P(), P(), P())
    return jax.shard_map(
        on_device,
        mesh=mesh,
        in_specs=placed,
        out_specs=(P("gz", "gy", None), P(None, "gy", "gz")),
        check_vma=False,
    )
```
